32 devices in a mesh: wide: 8 (over y, x, core), narrow: 4 (over z).
Axes of the slice: x: 2, y: 2, z: 4, core: 2. Of those that a mesh axis runs over, the one named last changes fastest.
Arguments:
- row_vectors: bfloat16 [8192, 2048], P('wide'), may hold values from -0.59765625 to 1.3984375
- col_vectors: bfloat16 [2048, 2048], P('narrow', 'wide'), may hold values from -0.59765625 to 1.3984375
- primal_matrix: bfloat16 [2048, 2048], P('wide'), may hold values from -1 to 3, as said below
- dual_inverse: bfloat16 [2048, 2048], P('wide'), may hold values from -1 to 3, as said below
Outputs:
- factored: float32 [8192, 2048], P('wide', 'narrow')
The draws below stay inside these ranges and needn't reach their ends.
Inputs may be any that keep to these rules, and one draw needn't show every extreme that they name: `primal_matrix`: symmetric positive definite. `dual_inverse`: symmetric positive definite.
All inputs are finite; a program needn't handle non-finite values.
Results may differ from the reference program's by a relative error of at most 0.0027.
Values may be sent and summed in bfloat16 or wider, within the bound.
No kernel may reach another device: no remote copies, remote signals or barrier semaphores. Data moves between devices by JAX's collectives and lax.ppermute only.
A program may use at most 64 MiB of HBM per device.

```python
import math
import jax
import jax.numpy as jnp
from jax import lax

N = 2048
PANEL = 512
ROWS = 8192
COLS = 2048


def draw_definite(key, salt_value):
    base_key = jax.random.fold_in(key, salt_value)
    key_diag, key_off = jax.random.split(base_key)
    diag_values = jnp.exp(jax.random.uniform(key_diag, (N,), jnp.float32, math.log(0.6), math.log(2.4)))
    off_part = jax.random.normal(key_off, (N, N), jnp.float32) * (0.25 / math.sqrt(N))
    sym_part = (off_part + off_part.T) * 0.5
    return (jnp.diag(diag_values) + sym_part).astype(jnp.bfloat16)


def draw_primal_matrix(key, part):
    return draw_definite(key, 11)


def draw_dual_inverse(key, part):
    return draw_definite(key, 23)


def level_of(stream_key, dims, cuts, least, largest):
    def one(position, blocks):
        steps = jax.random.uniform(jax.random.fold_in(jax.random.fold_in(stream_key, 6), position), (blocks,), jnp.float32, least / len(cuts), largest / len(cuts))
        return jnp.repeat(jnp.exp(steps), dims[position] // blocks).reshape((-1,) + (1,) * (len(dims) - position - 1))

    factor_of = one(*cuts[0])
    for cut in cuts[1:]:
        factor_of = factor_of * one(*cut)
    return factor_of


def setup_inputs(seed: int = 0) -> dict:
    seeds = jax.random.split(jax.random.key(seed), 5)
    row_vectors = jnp.clip(-0.59765625 + 1.9960938 * jax.random.uniform(seeds[0], (ROWS, N), jnp.float32) ** level_of(seeds[0], (ROWS, N), ((0, 8),), -0.2, 0.2), -0.59765625, 1.3984375).astype(jnp.bfloat16)
    col_vectors = jnp.clip(-0.59765625 + 1.9960938 * jax.random.uniform(seeds[1], (COLS, N), jnp.float32) ** level_of(seeds[1], (COLS, N), ((0, 4), (1, 8)), -0.2, 0.2), -0.59765625, 1.3984375).astype(jnp.bfloat16)
    primal_matrix = draw_primal_matrix(jax.random.fold_in(seeds[4], 71), 0)
    dual_inverse = draw_dual_inverse(jax.random.fold_in(seeds[4], 71), 0)
    return {"row_vectors": row_vectors, "col_vectors": col_vectors, "primal_matrix": primal_matrix, "dual_inverse": dual_inverse}


def reference(row_vectors, col_vectors, primal_matrix, dual_inverse):
    cone_order = primal_matrix.shape[0]
    gram_scale = 16.0 / (cone_order * cone_order)
    prod_primal = jnp.dot(primal_matrix.astype(jnp.float32), col_vectors.T.astype(jnp.float32), preferred_element_type=jnp.float32).astype(jnp.bfloat16)
    prod_dual = jnp.dot(dual_inverse.astype(jnp.float32), col_vectors.T.astype(jnp.float32), preferred_element_type=jnp.float32).astype(jnp.bfloat16)
    gram_primal = jnp.dot(row_vectors.astype(jnp.float32), prod_primal.astype(jnp.float32), preferred_element_type=jnp.float32)
    gram_dual = jnp.dot(row_vectors.astype(jnp.float32), prod_dual.astype(jnp.float32), preferred_element_type=jnp.float32)
    slab = gram_primal * gram_dual * gram_scale
    panel_set = col_vectors[:PANEL]
    gram = jnp.dot(panel_set.astype(jnp.float32), prod_primal.astype(jnp.float32), preferred_element_type=jnp.float32) * jnp.dot(panel_set.astype(jnp.float32), prod_dual.astype(jnp.float32), preferred_element_type=jnp.float32) * gram_scale
    factor = jnp.linalg.cholesky(gram[:, :PANEL])
    solved = jax.scipy.linalg.solve_triangular(factor, gram, lower=True)
    panel_cols = jax.scipy.linalg.solve_triangular(factor, slab[:, :PANEL].T, lower=True).T
    trailing = slab[:, PANEL:] - jnp.dot(panel_cols, solved[:, PANEL:], precision=lax.Precision.HIGHEST)
    return jnp.concatenate([panel_cols, trailing], axis=1)
```

```python
import functools

import jax
import jax.numpy as jnp
from jax import lax
from jax.experimental import pallas as pl
from jax.experimental.pallas import tpu as pltpu
from jax.sharding import PartitionSpec as P

HIGHEST = lax.Precision.HIGHEST
HIGH = lax.Precision.HIGH
NT = (((1,), (1,)), ((), ()))
TN = (((0,), (0,)), ((), ()))


def after(value, *earlier):
    return lax.optimization_barrier((value,) + earlier)[0]


def swap(value, mask, count):
    return lax.ppermute(value, "wide", [(i, i ^ mask) for i in range(count)])


def gather_pieces(value, count):
    pieces = [value] + [None] * (count - 1)
    for mask in range(2, count, 2):
        pieces[mask] = swap(value, mask, count)
    for mask in range(1, count, 2):
        pieces[mask] = swap(pieces[mask - 1], 1, count)
    return pieces


def place(pieces, axis):
    me = lax.axis_index("wide")
    size = pieces[0].shape[axis]
    shape = list(pieces[0].shape)
    shape[axis] = size * len(pieces)
    whole = jnp.zeros(shape, pieces[0].dtype)
    for mask, piece in enumerate(pieces):
        whole = lax.dynamic_update_slice_in_dim(whole, piece, (me ^ mask) * size, axis)
    return whole


def from_first(value):
    count = lax.axis_size("narrow")
    total = jnp.where(lax.axis_index("narrow") == 0, value, 0).astype(value.dtype)
    for target in range(1, count):
        total = total + lax.ppermute(value, "narrow", [(0, target)])
    return total


def eliminate(block):
    size = block.shape[0]
    groups = size // 8
    rows = lax.broadcasted_iota(jnp.int32, (8, size), 0)
    lanes = lax.broadcasted_iota(jnp.int32, (8, size), 1)
    left = [block[8 * i : 8 * i + 8] for i in range(groups)]
    right = [jnp.where(lanes == rows + 8 * i, 1.0, 0.0).astype(jnp.float32) for i in range(groups)]

    def column(value, j):
        return jnp.broadcast_to(value[:, j : j + 1], (8, size))

    def row(value, i):
        return jnp.broadcast_to(value[i : i + 1, :], (8, size))

    pivots = []
    current = [column(left[i], 0) for i in range(groups)]
    for j in range(size):
        group, inner = j // 8, j % 8
        pivot = row(current[group], inner)
        pivots.append(pivot)
        if j == size - 1:
            break
        inverse = 1.0 / pivot
        left_row = row(left[group], inner) * inverse
        right_row = row(right[group], inner) * inverse
        below = {
            i: current[i] if i > group else jnp.where(rows > inner, current[i], 0.0)
            for i in range(group, groups)
        }
        ahead = {i: column(left[i], j + 1) for i in range(group, groups)}
        step = row(ahead[group], inner) * inverse
        for i in range(group, groups):
            current[i] = ahead[i] - below[i] * step
        for i in range(group, groups):
            if i == group and inner == 7:
                continue
            left[i] = left[i] - below[i] * left_row
            right[i] = right[i] - below[i] * right_row
    out = []
    for i in range(groups):
        pivot = pivots[8 * i]
        for q in range(1, 8):
            pivot = jnp.where(rows == q, pivots[8 * i + q], pivot)
        out.append(right[i] * lax.rsqrt(pivot))
    return jnp.concatenate(out, axis=0)


def inverse_kernel(size, gram_ref, out_ref, work, line):
    order = gram_ref.shape[0]
    gram = gram_ref[...]
    work[:, :order] = (gram + gram.T) * 0.5
    work[:, order:] = jnp.where(
        lax.broadcasted_iota(jnp.int32, (order, order), 0)
        == lax.broadcasted_iota(jnp.int32, (order, order), 1),
        1.0,
        0.0,
    ).astype(jnp.float32)
    for start in range(0, order, size):
        stop = start + size
        inverse = eliminate(work[start:stop, start:stop])
        line[...] = jnp.dot(
            inverse, work[start:stop, :], precision=HIGHEST, preferred_element_type=jnp.float32
        )
        out_ref[start:stop, :] = line[:, order:]
        if stop < order:
            work[stop:, stop : order + stop] -= lax.dot_general(
                line[:, stop:order],
                line[:, stop : order + stop],
                TN,
                precision=HIGHEST,
                preferred_element_type=jnp.float32,
            )


def factor_inverse(gram):
    order = gram.shape[0]
    size = 128
    vmem = pl.BlockSpec(memory_space=pltpu.VMEM)
    return pl.pallas_call(
        functools.partial(inverse_kernel, size),
        out_shape=jax.ShapeDtypeStruct((order, order), jnp.float32),
        in_specs=[vmem],
        out_specs=vmem,
        scratch_shapes=[
            pltpu.VMEM((order, 2 * order), jnp.float32),
            pltpu.VMEM((size, 2 * order), jnp.float32),
        ],
        cost_estimate=pl.CostEstimate(
            flops=30_000_000_000, transcendentals=order, bytes_accessed=8 * order * order
        ),
        name="factor_inverse",
    )(gram)


def dot_nt(left, right, precision=None):
    return lax.dot_general(
        left, right, NT, precision=precision, preferred_element_type=jnp.float32
    )


def per_device(row_vectors, col_vectors, primal_matrix, dual_inverse):
    wide_count = lax.axis_size("wide")
    narrow_index = lax.axis_index("narrow")
    cone_order = primal_matrix.shape[1]
    gram_scale = 16.0 / (cone_order * cone_order)

    columns = place(gather_pieces(col_vectors, wide_count), 1)
    products = jnp.stack(
        [
            dot_nt(columns, primal_matrix).astype(jnp.bfloat16),
            dot_nt(columns, dual_inverse).astype(jnp.bfloat16),
        ]
    )
    share = lax.all_to_all(products, "wide", 1, 2, tiled=True)
    diag_share = dot_nt(share[0], columns) * dot_nt(share[1], columns) * gram_scale
    diag_share = from_first(diag_share)
    products = after(products, diag_share)
    diag = place(gather_pieces(diag_share, wide_count), 0)
    first = from_first(products)
    own_pieces = gather_pieces(products, wide_count)
    own = place(own_pieces, 2)
    first = place(gather_pieces(first, wide_count), 2)
    inverse = factor_inverse(diag)
    slab = dot_nt(row_vectors, own[0]) * dot_nt(row_vectors, own[1]) * gram_scale
    slab_first = dot_nt(row_vectors, first[0]) * dot_nt(row_vectors, first[1]) * gram_scale
    gram = dot_nt(first[0], columns) * dot_nt(first[1], columns) * gram_scale
    panel_cols = dot_nt(slab_first, inverse, HIGH)
    solved = jnp.dot(inverse, gram, precision=HIGH)
    trailing = slab - jnp.dot(panel_cols, solved, precision=HIGH)
    return jnp.where(narrow_index == 0, panel_cols, trailing)


def solution(mesh):
    placed = (P("wide", None), P("narrow", "wide"), P("wide", None), P("wide", None))
    return jax.shard_map(
        per_device, mesh=mesh, in_specs=placed, out_specs=P("wide", "narrow"), check_vma=False
    )
```

```python
import functools

import jax
import jax.numpy as jnp
from jax import lax
from jax.experimental import pallas as pl
from jax.experimental.pallas import tpu as pltpu
from jax.sharding import PartitionSpec as P

HIGHEST = lax.Precision.HIGHEST
NN = (((1,), (0,)), ((), ()))
NT = (((1,), (1,)), ((), ()))
TN = (((0,), (0,)), ((), ()))
VMEM = pl.BlockSpec(memory_space=pltpu.VMEM)
SMEM = pl.BlockSpec(memory_space=pltpu.SMEM)


def after(value, *earlier):
    return lax.optimization_barrier((value,) + earlier)[0]


def swap(value, mask, count):
    return lax.ppermute(value, "wide", [(i, i ^ mask) for i in range(count)])


def forward(pieces, mask, count):
    high = 1 << (mask.bit_length() - 1)
    low = mask & -mask
    if high == low:
        return swap(pieces[0], mask, count)
    even = lax.axis_index("wide") % 2 == 0
    held = jnp.where(even, pieces[mask ^ high], pieces[mask ^ low])
    return lax.ppermute(held, "wide", [(i, i ^ (low if i % 2 else high)) for i in range(count)])


def gather_pieces(value, count):
    pieces = [value] + [None] * (count - 1)
    masks = sorted(range(2, count, 2), key=lambda m: (bin(m).count("1"), m))
    for mask in masks:
        pieces[mask] = forward(pieces, mask, count)
    for mask in range(1, count, 2):
        pieces[mask] = swap(pieces[mask - 1], 1, count)
    return pieces


def from_first(value):
    count = lax.axis_size("narrow")
    total = jnp.where(lax.axis_index("narrow") == 0, value, 0).astype(value.dtype)
    for target in range(1, count):
        total = total + lax.ppermute(value, "narrow", [(0, target)])
    return total


def dot(left, right, dims=NN, precision=None):
    return lax.dot_general(
        left, right, dims, precision=precision, preferred_element_type=jnp.float32
    )


def halves(value):
    high = value.astype(jnp.bfloat16)
    return high, (value - high.astype(jnp.float32)).astype(jnp.bfloat16)


def dot_halves(left, right, dims):
    left_high, left_low = left
    right_high, right_low = right
    return dot(left_high, right_high, dims) + (
        dot(left_high, right_low, dims) + dot(left_low, right_high, dims)
    )


def eliminate(block):
    size = block.shape[0]
    groups = size // 8
    rows = lax.broadcasted_iota(jnp.int32, (8, size), 0)
    lanes = lax.broadcasted_iota(jnp.int32, (8, size), 1)
    left = [block[8 * i : 8 * i + 8] for i in range(groups)]
    right = [jnp.where(lanes == rows + 8 * i, 1.0, 0.0).astype(jnp.float32) for i in range(groups)]

    def column(value, j):
        return jnp.broadcast_to(value[:, j : j + 1], (8, size))

    def row(value, i):
        return jnp.broadcast_to(value[i : i + 1, :], (8, size))

    pivots = [None] * size
    first = {i: column(left[i], 0) for i in range(groups)}
    second = {i: column(left[i], 1) for i in range(groups)}
    for j in range(0, size, 2):
        g, r = j // 8, j % 8
        top = row(first[g], r)
        side = row(first[g], r + 1)
        minor = top * row(second[g], r + 1) - side * side
        top_inverse = 1.0 / top
        factor = side * top_inverse
        low_inverse = top * (1.0 / minor)
        pivots[j] = top
        pivots[j + 1] = minor * top_inverse
        left_top = row(left[g], r)
        left_low = (row(left[g], r + 1) - factor * left_top) * low_inverse
        left_top = left_top * top_inverse
        right_top = row(right[g], r)
        right_next = row(right[g], r + 1) - factor * right_top
        right_low = right_next * low_inverse
        right_top = right_top * top_inverse
        a, b = {}, {}
        for i in range(g, groups):
            if i > g:
                a[i], b[i] = first[i], second[i] - first[i] * factor
            elif r < 6:
                below = rows > r + 1
                a[i] = jnp.where(below, first[i], 0.0)
                b[i] = jnp.where(below, second[i] - first[i] * factor, 0.0)
        if j + 2 < size:
            ahead = [{}, {}]
            for q in range(2):
                lead = column(left[g], j + 2 + q)
                high = row(lead, r)
                low = (row(lead, r + 1) - factor * high) * low_inverse
                high = high * top_inverse
                for i in range((j + 2) // 8, groups):
                    value = lead if i == g else column(left[i], j + 2 + q)
                    ahead[q][i] = value - a[i] * high - b[i] * low
            first, second = ahead
        right[g] = jnp.where(rows == r + 1, right_next, right[g])
        for i in a:
            left[i] = left[i] - a[i] * left_top - b[i] * left_low
            right[i] = right[i] - a[i] * right_top - b[i] * right_low
    out = []
    for i in range(groups):
        pivot = pivots[8 * i]
        for q in range(1, 8):
            pivot = jnp.where(rows == q, pivots[8 * i + q], pivot)
        out.append(right[i] * lax.rsqrt(pivot))
    return jnp.concatenate(out, axis=0)


def block_of(ref, me_ref, mask, size):
    if size % 128:
        return ref[:, mask * size : (mask + 1) * size]
    return ref[:, pl.ds(pl.multiple_of((me_ref[0] ^ mask) * size, size), size)]


def products_kernel(me_ref, primal_ref, dual_ref, *refs):
    pieces, out_ref = refs[:-1], refs[-1]
    size = primal_ref.shape[0]
    for which, ref in enumerate((primal_ref, dual_ref)):
        total = None
        for mask, piece in enumerate(pieces):
            part = dot(block_of(ref, me_ref, mask, size), piece[...], NT)
            total = part if total is None else total + part
        out_ref[which] = total.astype(out_ref.dtype)


def products(me, primal, dual, pieces):
    size, width = primal.shape[0], pieces[0].shape[0]
    return pl.pallas_call(
        products_kernel,
        out_shape=jax.ShapeDtypeStruct((2, size, width), jnp.bfloat16),
        in_specs=[SMEM] + [VMEM] * (2 + len(pieces)),
        out_specs=VMEM,
        name="products",
    )(me, primal, dual, *pieces)


def summed(lines, sides, which):
    total = None
    for line, side in zip(lines, sides):
        part = dot(line[...], side[which])
        total = part if total is None else total + part
    return total


def accumulate_kernel(count, fresh, *refs):
    lines, sides, out_ref = refs[:count], refs[count : 2 * count], refs[-1]
    for which in range(2):
        total = summed(lines, sides, which)
        out_ref[which] = total if fresh else refs[2 * count][which] + total


def accumulate(lines, sides, earlier=None):
    tile = 256
    depth = lines[0].shape[1]
    height, width = lines[0].shape[0], sides[0].shape[2]
    line = pl.BlockSpec((tile, depth), lambda i: (i, 0))
    side = pl.BlockSpec((2, depth, width), lambda i: (0, 0, 0))
    total = pl.BlockSpec((2, tile, width), lambda i: (0, i, 0))
    count = len(lines)
    more = [] if earlier is None else [earlier]
    return pl.pallas_call(
        functools.partial(accumulate_kernel, count, earlier is None),
        grid=(height // tile,),
        out_shape=jax.ShapeDtypeStruct((2, height, width), jnp.float32),
        in_specs=[line] * count + [side] * count + [total] * len(more),
        out_specs=total,
        input_output_aliases={2 * count: 0} if more else {},
        name="accumulate",
    )(*lines, *sides, *more)


def inverse_kernel(size, scale, count, *refs):
    lines, sides = refs[:count], refs[count : 2 * count]
    total_ref, out_ref, work, line = refs[2 * count :]
    order = out_ref.shape[0]
    gram = (
        (total_ref[0] + summed(lines, sides, 0)) * (total_ref[1] + summed(lines, sides, 1)) * scale
    )
    work[:, :order] = (gram + gram.T) * 0.5
    work[:, order:] = jnp.where(
        lax.broadcasted_iota(jnp.int32, (order, order), 0)
        == lax.broadcasted_iota(jnp.int32, (order, order), 1),
        1.0,
        0.0,
    ).astype(jnp.float32)
    for start in range(0, order, size):
        stop = start + size
        inverse = eliminate(work[start:stop, start:stop])
        line[:, start : order + stop] = dot(
            inverse, work[start:stop, start : order + stop], NN, HIGHEST
        )
        out_ref[start:stop, :stop] = line[:, order : order + stop]
        if stop < order:
            out_ref[start:stop, stop:] = jnp.zeros((size, order - stop), jnp.float32)
            work[stop:, stop : order + stop] -= dot(
                line[:, stop:order], line[:, stop : order + stop], TN, HIGHEST
            )


def factor_inverse(total, lines, sides, scale):
    size = 128
    count, depth = len(lines), lines[0].shape[1]
    order = sides[0].shape[2]
    return pl.pallas_call(
        functools.partial(inverse_kernel, size, scale, count),
        grid=(1,),
        out_shape=jax.ShapeDtypeStruct((order, order), jnp.float32),
        in_specs=[pl.BlockSpec((order, depth), lambda i: (0, 0))] * count
        + [pl.BlockSpec((2, depth, order), lambda i: (0, 0, 0))] * count
        + [pl.BlockSpec((2, order, order), lambda i: (0, 0, 0))],
        out_specs=pl.BlockSpec((order, order), lambda i: (0, 0)),
        scratch_shapes=[
            pltpu.VMEM((order, 2 * order), jnp.float32),
            pltpu.VMEM((size, 2 * order), jnp.float32),
        ],
        cost_estimate=pl.CostEstimate(
            flops=15_000_000_000, transcendentals=order, bytes_accessed=8 * order * order
        ),
        name="factor_inverse",
    )(*lines, *sides, total)


def project_kernel(scale, count, *refs):
    lines, sides = refs[:count], refs[count : 2 * count]
    total_ref, inverse_ref, out_ref = refs[2 * count :]
    value = (
        (total_ref[0] + summed(lines, sides, 0)) * (total_ref[1] + summed(lines, sides, 1)) * scale
    )
    half = inverse_ref.shape[0] // 2
    left = halves(value)
    right = halves(inverse_ref[...])
    out_ref[:, :half] = dot_halves(
        [v[:, :half] for v in left], [v[:half, :half] for v in right], NT
    )
    out_ref[:, half:] = dot_halves(left, [v[half:] for v in right], NT)


def project(total, lines, sides, inverse, scale):
    tile = 256
    count, depth = len(lines), lines[0].shape[1]
    height, width = lines[0].shape[0], sides[0].shape[2]
    skip = width // tile
    line = pl.BlockSpec((tile, depth), lambda i: (i + skip, 0))
    return pl.pallas_call(
        functools.partial(project_kernel, scale, count),
        grid=(height // tile - skip,),
        out_shape=jax.ShapeDtypeStruct((height - width, width), jnp.float32),
        in_specs=[line] * count
        + [pl.BlockSpec((2, depth, width), lambda i: (0, 0, 0))] * count
        + [
            pl.BlockSpec((2, tile, width), lambda i: (0, i + skip, 0)),
            pl.BlockSpec((width, width), lambda i: (0, 0)),
        ],
        out_specs=pl.BlockSpec((tile, width), lambda i: (i, 0)),
        name="project",
    )(*lines, *sides, total, inverse)


def update_kernel(scale, count, narrow_ref, *refs):
    lines, sides = refs[:count], refs[count : 2 * count]
    panel_ref, solved_ref, out_ref = refs[2 * count :]
    slab = summed(lines, sides, 0) * summed(lines, sides, 1) * scale
    panel = panel_ref[...]
    trailing = slab - dot_halves(halves(panel), halves(solved_ref[...]), NT)
    out_ref[...] = jnp.where(narrow_ref[0] == 0, panel, trailing)


def update(narrow, lines, sides, projected, scale):
    tile = 256
    count, depth = len(lines), lines[0].shape[1]
    width = sides[0].shape[2]
    solved_height = width
    height = projected.shape[0] - solved_height
    skip = (lines[0].shape[0] - height) // tile
    ahead = solved_height // tile
    return pl.pallas_call(
        functools.partial(update_kernel, scale, count),
        grid=(height // tile,),
        out_shape=jax.ShapeDtypeStruct((height, width), jnp.float32),
        in_specs=[SMEM]
        + [pl.BlockSpec((tile, depth), lambda i: (i + skip, 0))] * count
        + [pl.BlockSpec((2, depth, width), lambda i: (0, 0, 0))] * count
        + [
            pl.BlockSpec((tile, width), lambda i: (i + ahead, 0)),
            pl.BlockSpec((solved_height, width), lambda i: (0, 0)),
        ],
        out_specs=pl.BlockSpec((tile, width), lambda i: (i, 0)),
        name="update",
    )(narrow, *lines, *sides, projected, projected)


def per_device(row_vectors, col_vectors, primal_matrix, dual_inverse):
    count = lax.axis_size("wide")
    me = lax.axis_index("wide")
    share, cone_order = primal_matrix.shape
    scale = 16.0 / (cone_order * cone_order)

    def block(value, mask):
        return lax.dynamic_slice_in_dim(value, (me ^ mask) * share, share, 1)

    if share % 128:
        primal_matrix, dual_inverse = (
            jnp.concatenate([block(v, mask) for mask in range(count)], axis=1)
            for v in (primal_matrix, dual_inverse)
        )
    where = jnp.reshape(me, (1,)).astype(jnp.int32)
    narrow = jnp.reshape(lax.axis_index("narrow"), (1,)).astype(jnp.int32)

    panel = from_first(col_vectors)
    col_pieces = gather_pieces(col_vectors, count)
    panel_pieces = gather_pieces(panel, count)
    first = products(where, primal_matrix, dual_inverse, panel_pieces)
    first_pieces = gather_pieces(first, count)
    lines = [
        jnp.concatenate([panel_pieces[m], col_pieces[m], block(row_vectors, m)], axis=0)
        for m in range(count)
    ]
    total = accumulate(lines[:2], first_pieces[:2])
    total = accumulate(lines[2:-2], first_pieces[2:-2], total)

    own = products(where, primal_matrix, dual_inverse, col_pieces)
    own = after(own, first_pieces[-2])
    own_pieces = [own] + [None] * (count - 1)
    for mask in range(2, count, 2):
        own_pieces[mask] = swap(own, mask, count)
    inverse = factor_inverse(total, lines[-2:], first_pieces[-2:], scale)
    for mask in range(0, count, 2):
        held = own_pieces[mask]
        own_pieces[mask + 1] = swap(after(held, inverse) if mask else held, 1, count)

    projected = project(total, lines[-2:], first_pieces[-2:], inverse, scale)
    return update(narrow, lines, own_pieces, projected, scale)


def solution(mesh):
    placed = (P("wide", None), P("narrow", "wide"), P("wide", None), P("wide", None))
    return jax.shard_map(
        per_device, mesh=mesh, in_specs=placed, out_specs=P("wide", "narrow"), check_vma=False
    )
```

```python
import functools

import jax
import jax.numpy as jnp
from jax import lax
from jax.experimental import pallas as pl
from jax.experimental.pallas import tpu as pltpu
from jax.sharding import PartitionSpec as P

HIGHEST = lax.Precision.HIGHEST
NN = (((1,), (0,)), ((), ()))
NT = (((1,), (1,)), ((), ()))
TN = (((0,), (0,)), ((), ()))
VMEM = pl.BlockSpec(memory_space=pltpu.VMEM)
SMEM = pl.BlockSpec(memory_space=pltpu.SMEM)


def after(value, *earlier):
    return lax.optimization_barrier((value,) + earlier)[0]


def swap(value, mask, count):
    return lax.ppermute(value, "wide", [(i, i ^ mask) for i in range(count)])


def forward(pieces, mask, count):
    high = 1 << (mask.bit_length() - 1)
    low = mask & -mask
    if high == low:
        return swap(pieces[0], mask, count)
    even = lax.axis_index("wide") % 2 == 0
    held = jnp.where(even, pieces[mask ^ high], pieces[mask ^ low])
    return lax.ppermute(held, "wide", [(i, i ^ (low if i % 2 else high)) for i in range(count)])


def gather_pieces(value, count):
    pieces = [value] + [None] * (count - 1)
    masks = sorted(range(2, count, 2), key=lambda m: (bin(m).count("1"), m))
    for mask in masks:
        pieces[mask] = forward(pieces, mask, count)
    for mask in range(1, count, 2):
        pieces[mask] = swap(pieces[mask - 1], 1, count)
    return pieces


def from_first(value):
    count = lax.axis_size("narrow")
    total = jnp.where(lax.axis_index("narrow") == 0, value, 0).astype(value.dtype)
    for target in range(1, count):
        total = total + lax.ppermute(value, "narrow", [(0, target)])
    return total


def dot(left, right, dims=NN, precision=None):
    return lax.dot_general(
        left, right, dims, precision=precision, preferred_element_type=jnp.float32
    )


def halves(value):
    high = value.astype(jnp.bfloat16)
    return high, (value - high.astype(jnp.float32)).astype(jnp.bfloat16)


def dot_halves(left, right, dims):
    left_high, left_low = left
    right_high, right_low = right
    return dot(left_high, right_high, dims) + (
        dot(left_high, right_low, dims) + dot(left_low, right_high, dims)
    )


def eliminate(block):
    size = block.shape[0]
    groups = size // 8
    rows = lax.broadcasted_iota(jnp.int32, (8, size), 0)
    lanes = lax.broadcasted_iota(jnp.int32, (8, size), 1)
    left = [block[8 * i : 8 * i + 8] for i in range(groups)]
    right = [jnp.where(lanes == rows + 8 * i, 1.0, 0.0).astype(jnp.float32) for i in range(groups)]

    def column(value, j):
        return jnp.broadcast_to(value[:, j : j + 1], (8, size))

    def row(value, i):
        return jnp.broadcast_to(value[i : i + 1, :], (8, size))

    pivots = [None] * size
    first = {i: column(left[i], 0) for i in range(groups)}
    second = {i: column(left[i], 1) for i in range(groups)}
    for j in range(0, size, 2):
        g, r = j // 8, j % 8
        top = row(first[g], r)
        side = row(first[g], r + 1)
        minor = top * row(second[g], r + 1) - side * side
        top_inverse = 1.0 / top
        factor = side * top_inverse
        low_inverse = top * (1.0 / minor)
        pivots[j] = top
        pivots[j + 1] = minor * top_inverse
        left_top = row(left[g], r)
        left_low = (row(left[g], r + 1) - factor * left_top) * low_inverse
        left_top = left_top * top_inverse
        right_top = row(right[g], r)
        right_next = row(right[g], r + 1) - factor * right_top
        right_low = right_next * low_inverse
        right_top = right_top * top_inverse
        a, b = {}, {}
        for i in range(g, groups):
            if i > g:
                a[i], b[i] = first[i], second[i] - first[i] * factor
            elif r < 6:
                below = rows > r + 1
                a[i] = jnp.where(below, first[i], 0.0)
                b[i] = jnp.where(below, second[i] - first[i] * factor, 0.0)
        if j + 2 < size:
            ahead = [{}, {}]
            for q in range(2):
                lead = column(left[g], j + 2 + q)
                high = row(lead, r)
                low = (row(lead, r + 1) - factor * high) * low_inverse
                high = high * top_inverse
                for i in range((j + 2) // 8, groups):
                    value = lead if i == g else column(left[i], j + 2 + q)
                    ahead[q][i] = value - a[i] * high - b[i] * low
            first, second = ahead
        right[g] = jnp.where(rows == r + 1, right_next, right[g])
        for i in a:
            left[i] = left[i] - a[i] * left_top - b[i] * left_low
            right[i] = right[i] - a[i] * right_top - b[i] * right_low
    out = []
    for i in range(groups):
        pivot = pivots[8 * i]
        for q in range(1, 8):
            pivot = jnp.where(rows == q, pivots[8 * i + q], pivot)
        out.append(right[i] * lax.rsqrt(pivot))
    return jnp.concatenate(out, axis=0)


def block_of(ref, me_ref, mask, size):
    if size % 128:
        return ref[:, mask * size : (mask + 1) * size]
    return ref[:, pl.ds(pl.multiple_of((me_ref[0] ^ mask) * size, size), size)]


def products_kernel(me_ref, primal_ref, dual_ref, *refs):
    pieces, out_ref = refs[:-1], refs[-1]
    size = primal_ref.shape[0]
    for which, ref in enumerate((primal_ref, dual_ref)):
        total = None
        for mask, piece in enumerate(pieces):
            part = dot(block_of(ref, me_ref, mask, size), piece[...], NT)
            total = part if total is None else total + part
        out_ref[which] = total.astype(out_ref.dtype)


def products(me, primal, dual, pieces):
    size, width = primal.shape[0], pieces[0].shape[0]
    return pl.pallas_call(
        products_kernel,
        out_shape=jax.ShapeDtypeStruct((2, size, width), jnp.bfloat16),
        in_specs=[SMEM] + [VMEM] * (2 + len(pieces)),
        out_specs=VMEM,
        name="products",
    )(me, primal, dual, *pieces)


def summed(lines, sides, which):
    total = None
    for line, side in zip(lines, sides):
        part = dot(line[...], side[which])
        total = part if total is None else total + part
    return total


def row_lines(rows, me, share, tile, masks):
    if share % 128:
        arrays = [
            lax.dynamic_slice_in_dim(rows, (me[0] ^ mask) * share, share, 1) for mask in masks
        ]
        return arrays, [pl.BlockSpec((tile, share), lambda i, s: (i, 0))] * len(masks)
    specs = [
        pl.BlockSpec((tile, share), lambda i, s, mask=mask: (i, s[0] ^ mask)) for mask in masks
    ]
    return [rows] * len(masks), specs


def piece_lines(pieces, tile, masks):
    share = pieces[0].shape[1]
    spec = pl.BlockSpec((tile, share), lambda i, s: (i, 0))
    return [pieces[mask] for mask in masks], [spec] * len(masks)


def side_specs(sides):
    return [pl.BlockSpec(side.shape, lambda i, s: (0, 0, 0)) for side in sides]


def call(kernel, steps, scalars, operands, specs, out_shape, out_spec, **more):
    scratch = more.pop("scratch_shapes", ())
    return pl.pallas_call(
        kernel,
        grid_spec=pltpu.PrefetchScalarGridSpec(
            num_scalar_prefetch=1,
            grid=(steps,),
            in_specs=specs,
            out_specs=out_spec,
            scratch_shapes=scratch,
        ),
        out_shape=out_shape,
        **more,
    )(scalars, *operands)


def accumulate_kernel(count, fresh, scalars, *refs):
    lines, sides, out_ref = refs[:count], refs[count : 2 * count], refs[-1]
    for which in range(2):
        total = summed(lines, sides, which)
        out_ref[which] = total if fresh else refs[2 * count][which] + total


def accumulate(scalars, height, tile, lines, sides, earlier=None):
    arrays, specs = lines
    width = sides[0].shape[2]
    total = pl.BlockSpec((2, tile, width), lambda i, s: (0, i, 0))
    count = len(arrays)
    more = [] if earlier is None else [earlier]
    return call(
        functools.partial(accumulate_kernel, count, earlier is None),
        height // tile,
        scalars,
        [*arrays, *sides, *more],
        specs + side_specs(sides) + [total] * len(more),
        jax.ShapeDtypeStruct((2, height, width), jnp.float32),
        total,
        input_output_aliases={2 * count + 1: 0} if more else {},
    )


def inverse_kernel(size, scale, count, scalars, *refs):
    lines, sides = refs[:count], refs[count : 2 * count]
    total_ref, out_ref, work, line = refs[2 * count :]
    order = out_ref.shape[1]
    gram = (
        (total_ref[0] + summed(lines, sides, 0)) * (total_ref[1] + summed(lines, sides, 1)) * scale
    )
    work[:, :order] = (gram + gram.T) * 0.5
    work[:, order:] = jnp.where(
        lax.broadcasted_iota(jnp.int32, (order, order), 0)
        == lax.broadcasted_iota(jnp.int32, (order, order), 1),
        1.0,
        0.0,
    ).astype(jnp.float32)
    for start in range(0, order, size):
        stop = start + size
        inverse = eliminate(work[start:stop, start:stop])
        line[:, start : order + stop] = dot(
            inverse, work[start:stop, start : order + stop], NN, HIGHEST
        )
        out_ref[0, start:stop, :stop], out_ref[1, start:stop, :stop] = halves(
            line[:, order : order + stop]
        )
        if stop < order:
            out_ref[:, start:stop, stop:] = jnp.zeros((2, size, order - stop), out_ref.dtype)
            work[stop:, stop : order + stop] -= dot(
                line[:, stop:order], line[:, stop : order + stop], TN, HIGHEST
            )


def factor_inverse(scalars, total, lines, sides, scale):
    size = 128
    arrays, specs = lines
    order = sides[0].shape[2]
    return call(
        functools.partial(inverse_kernel, size, scale, len(arrays)),
        1,
        scalars,
        [*arrays, *sides, total],
        specs + side_specs(sides + [total]),
        jax.ShapeDtypeStruct((2, order, order), jnp.bfloat16),
        pl.BlockSpec((2, order, order), lambda i, s: (0, 0, 0)),
        scratch_shapes=[
            pltpu.VMEM((order, 2 * order), jnp.float32),
            pltpu.VMEM((size, 2 * order), jnp.float32),
        ],
        cost_estimate=pl.CostEstimate(
            flops=15_000_000_000, transcendentals=order, bytes_accessed=8 * order * order
        ),
    )


def project_kernel(scale, count, fresh, scalars, *refs):
    lines, sides = refs[:count], refs[count : 2 * count]
    inverse_ref, out_ref = refs[2 * count], refs[-1]
    parts = [summed(lines, sides, which) for which in range(2)]
    if not fresh:
        parts = [part + refs[2 * count + 1][which] for which, part in enumerate(parts)]
    left = halves(parts[0] * parts[1] * scale)
    half = inverse_ref.shape[1] // 2
    low = dot_halves(
        [v[:, :half] for v in left], [inverse_ref[q, :half, :half] for q in range(2)], NT
    )
    high = dot_halves(left, [inverse_ref[q, half:, :] for q in range(2)], NT)
    if len(out_ref.shape) == 2:
        out_ref[:, :half] = low
        out_ref[:, half:] = high
    else:
        out_ref[0, :, :half], out_ref[1, :, :half] = halves(low)
        out_ref[0, :, half:], out_ref[1, :, half:] = halves(high)


def project(scalars, height, tile, lines, sides, inverse, scale, split, earlier=None):
    arrays, specs = lines
    width = sides[0].shape[2]
    count = len(arrays)
    both = pl.BlockSpec((2, tile, width), lambda i, s: (0, i, 0))
    more = [] if earlier is None else [earlier]
    if split:
        out = jax.ShapeDtypeStruct((2, height, width), jnp.bfloat16), both
    else:
        out = (
            jax.ShapeDtypeStruct((height, width), jnp.float32),
            pl.BlockSpec((tile, width), lambda i, s: (i, 0)),
        )
    return call(
        functools.partial(project_kernel, scale, count, earlier is None),
        height // tile,
        scalars,
        [*arrays, *sides, inverse, *more],
        specs + side_specs(sides + [inverse]) + [both] * len(more),
        *out,
    )


def update_kernel(scale, count, scalars, *refs):
    lines, sides = refs[:count], refs[count : 2 * count]
    panel_ref, solved_ref, out_ref = refs[2 * count :]
    slab = summed(lines, sides, 0) * summed(lines, sides, 1) * scale
    panel = panel_ref[...]
    trailing = slab - dot_halves(halves(panel), [solved_ref[q] for q in range(2)], NT)
    out_ref[...] = jnp.where(scalars[1] == 0, panel, trailing)


def update(scalars, height, tile, lines, sides, panel, solved, scale):
    arrays, specs = lines
    width = sides[0].shape[2]
    tiles = pl.BlockSpec((tile, width), lambda i, s: (i, 0))
    return call(
        functools.partial(update_kernel, scale, len(arrays)),
        height // tile,
        scalars,
        [*arrays, *sides, panel, solved],
        specs + side_specs(sides) + [tiles] + side_specs([solved]),
        jax.ShapeDtypeStruct((height, width), jnp.float32),
        tiles,
    )


def per_device(row_vectors, col_vectors, primal_matrix, dual_inverse):
    count = lax.axis_size("wide")
    me = lax.axis_index("wide")
    share, cone_order = primal_matrix.shape
    height = row_vectors.shape[0]
    order = col_vectors.shape[0]
    tile = 256
    scale = 16.0 / (cone_order * cone_order)
    scalars = jnp.stack([me, lax.axis_index("narrow")]).astype(jnp.int32)
    early, late, every = range(2, count - 2), range(count - 2, count), range(count)

    if share % 128:
        primal_matrix, dual_inverse = (
            jnp.concatenate(
                [
                    lax.dynamic_slice_in_dim(value, (me ^ mask) * share, share, 1)
                    for mask in every
                ],
                axis=1,
            )
            for value in (primal_matrix, dual_inverse)
        )

    def rows(masks):
        return row_lines(row_vectors, scalars, share, tile, masks)

    panel = from_first(col_vectors)
    columns = gather_pieces(col_vectors, count)
    panel = after(panel, *columns)
    own = products(scalars, primal_matrix, dual_inverse, columns)
    panels = gather_pieces(panel, count)
    first = products(scalars, primal_matrix, dual_inverse, [after(panels[0], own), *panels[1:]])

    masks = sorted(range(2, count, 2), key=lambda m: (bin(m).count("1"), m))
    firsts = [first] + [None] * (count - 1)
    firsts[1] = swap(first, 1, count)
    begun = False
    for mask in masks:
        if bin(mask).count("1") > 1 and not begun:
            begun = True
            start = accumulate(scalars, height, tile, rows((0, 1)), firsts[:2])
            for bit in masks:
                if bin(bit).count("1") == 1:
                    firsts[bit] = after(firsts[bit], start)
                    firsts[bit + 1] = swap(firsts[bit], 1, count)
        firsts[mask] = forward(firsts, mask, count)
    for mask in masks:
        if firsts[mask + 1] is None and mask != count - 2:
            firsts[mask + 1] = swap(firsts[mask], 1, count)
    total = accumulate(
        scalars, order, tile, piece_lines(panels, tile, range(count - 2)), firsts[:-2]
    )
    middle = accumulate(scalars, height, tile, rows(early), firsts[2:-2], start)
    firsts[-2] = after(firsts[-2], total, middle)
    firsts[-1] = swap(firsts[-2], 1, count)

    owns = [own] + [None] * (count - 1)
    delayed = after(own, firsts[-2])
    for mask in range(2, count, 2):
        owns[mask] = swap(delayed, mask, count)
    owns[1] = swap(delayed, 1, count)
    inverse = factor_inverse(scalars, total, piece_lines(panels, order, late), firsts[-2:], scale)
    for mask in range(2, count, 2):
        owns[mask + 1] = swap(after(owns[mask], inverse), 1, count)

    solved = project(
        scalars, order, tile, piece_lines(columns, tile, every), firsts, inverse, scale, True
    )
    panel_cols = project(
        scalars, height, tile, rows(late), firsts[-2:], inverse, scale, False, middle
    )
    return update(scalars, height, tile, rows(every), owns, panel_cols, solved, scale)


def solution(mesh):
    placed = (P("wide", None), P("narrow", "wide"), P("wide", None), P("wide", None))
    return jax.shard_map(
        per_device, mesh=mesh, in_specs=placed, out_specs=P("wide", "narrow"), check_vma=False
    )
```

```python
import functools

import jax
import jax.numpy as jnp
from jax import lax
from jax.experimental import pallas as pl
from jax.experimental.pallas import tpu as pltpu
from jax.sharding import PartitionSpec as P

HIGHEST = lax.Precision.HIGHEST
NN = (((1,), (0,)), ((), ()))
NT = (((1,), (1,)), ((), ()))
TN = (((0,), (0,)), ((), ()))
VMEM = pl.BlockSpec(memory_space=pltpu.VMEM)
SMEM = pl.BlockSpec(memory_space=pltpu.SMEM)


def after(value, *earlier):
    return lax.optimization_barrier((value,) + earlier)[0]


def swap(value, mask, count):
    return lax.ppermute(value, "wide", [(i, i ^ mask) for i in range(count)])


def forward(pieces, mask, count):
    high = 1 << (mask.bit_length() - 1)
    low = mask & -mask
    if high == low:
        return swap(pieces[0], mask, count)
    even = lax.axis_index("wide") % 2 == 0
    held = jnp.where(even, pieces[mask ^ high], pieces[mask ^ low])
    return lax.ppermute(held, "wide", [(i, i ^ (low if i % 2 else high)) for i in range(count)])


def gather_pieces(value, count):
    pieces = [value] + [None] * (count - 1)
    masks = sorted(range(2, count, 2), key=lambda m: (bin(m).count("1"), m))
    for mask in masks:
        pieces[mask] = forward(pieces, mask, count)
    for mask in range(1, count, 2):
        pieces[mask] = swap(pieces[mask - 1], 1, count)
    return pieces


def from_first(value):
    count = lax.axis_size("narrow")
    total = jnp.where(lax.axis_index("narrow") == 0, value, 0).astype(value.dtype)
    for target in range(1, count):
        total = total + lax.ppermute(value, "narrow", [(0, target)])
    return total


def dot(left, right, dims=NN, precision=None):
    return lax.dot_general(
        left, right, dims, precision=precision, preferred_element_type=jnp.float32
    )


def halves(value):
    high = value.astype(jnp.bfloat16)
    return high, (value - high.astype(jnp.float32)).astype(jnp.bfloat16)


def dot_halves(left, right, dims):
    left_high, left_low = left
    right_high, right_low = right
    return dot(left_high, right_high, dims) + (
        dot(left_high, right_low, dims) + dot(left_low, right_high, dims)
    )


def eliminate(block):
    size = block.shape[0]
    groups = size // 8
    rows = lax.broadcasted_iota(jnp.int32, (8, size), 0)
    lanes = lax.broadcasted_iota(jnp.int32, (8, size), 1)
    left = [block[8 * i : 8 * i + 8] for i in range(groups)]
    right = [jnp.where(lanes == rows + 8 * i, 1.0, 0.0).astype(jnp.float32) for i in range(groups)]

    def column(value, j):
        return jnp.broadcast_to(value[:, j : j + 1], (8, size))

    def row(value, i):
        return jnp.broadcast_to(value[i : i + 1, :], (8, size))

    pivots = [None] * size
    first = {i: column(left[i], 0) for i in range(groups)}
    second = {i: column(left[i], 1) for i in range(groups)}
    for j in range(0, size, 2):
        g, r = j // 8, j % 8
        top = row(first[g], r)
        side = row(first[g], r + 1)
        minor = top * row(second[g], r + 1) - side * side
        top_inverse = 1.0 / top
        factor = side * top_inverse
        low_inverse = top * (1.0 / minor)
        pivots[j] = top
        pivots[j + 1] = minor * top_inverse
        left_top = row(left[g], r)
        left_low = (row(left[g], r + 1) - factor * left_top) * low_inverse
        left_top = left_top * top_inverse
        right_top = row(right[g], r)
        right_next = row(right[g], r + 1) - factor * right_top
        right_low = right_next * low_inverse
        right_top = right_top * top_inverse
        a, b = {}, {}
        for i in range(g, groups):
            if i > g:
                a[i], b[i] = first[i], second[i] - first[i] * factor
            elif r < 6:
                below = rows > r + 1
                a[i] = jnp.where(below, first[i], 0.0)
                b[i] = jnp.where(below, second[i] - first[i] * factor, 0.0)
        if j + 2 < size:
            ahead = [{}, {}]
            for q in range(2):
                lead = column(left[g], j + 2 + q)
                high = row(lead, r)
                low = (row(lead, r + 1) - factor * high) * low_inverse
                high = high * top_inverse
                for i in range((j + 2) // 8, groups):
                    value = lead if i == g else column(left[i], j + 2 + q)
                    ahead[q][i] = value - a[i] * high - b[i] * low
            first, second = ahead
        right[g] = jnp.where(rows == r + 1, right_next, right[g])
        for i in a:
            left[i] = left[i] - a[i] * left_top - b[i] * left_low
            right[i] = right[i] - a[i] * right_top - b[i] * right_low
    out = []
    for i in range(groups):
        pivot = pivots[8 * i]
        for q in range(1, 8):
            pivot = jnp.where(rows == q, pivots[8 * i + q], pivot)
        out.append(right[i] * lax.rsqrt(pivot))
    return jnp.concatenate(out, axis=0)


def block_of(ref, me_ref, mask, size):
    if size % 128:
        return ref[:, mask * size : (mask + 1) * size]
    return ref[:, pl.ds(pl.multiple_of((me_ref[0] ^ mask) * size, size), size)]


def products_kernel(me_ref, primal_ref, dual_ref, *refs):
    pieces, out_ref = refs[:-1], refs[-1]
    size = primal_ref.shape[0]
    for which, ref in enumerate((primal_ref, dual_ref)):
        total = None
        for mask, piece in enumerate(pieces):
            part = dot(block_of(ref, me_ref, mask, size), piece[...], NT)
            total = part if total is None else total + part
        out_ref[which] = total.astype(out_ref.dtype)


def products(me, primal, dual, pieces):
    size, width = primal.shape[0], pieces[0].shape[0]
    return pl.pallas_call(
        products_kernel,
        out_shape=jax.ShapeDtypeStruct((2, size, width), jnp.bfloat16),
        in_specs=[SMEM] + [VMEM] * (2 + len(pieces)),
        out_specs=VMEM,
        name="products",
    )(me, primal, dual, *pieces)


def summed(lines, sides, which):
    total = None
    for line, side in zip(lines, sides):
        part = dot(line[...], side[which])
        total = part if total is None else total + part
    return total


def row_lines(rows, me, share, tile, masks):
    if share % 128:
        arrays = [
            lax.dynamic_slice_in_dim(rows, (me[0] ^ mask) * share, share, 1) for mask in masks
        ]
        return arrays, [pl.BlockSpec((tile, share), lambda i, s: (i, 0))] * len(masks)
    specs = [
        pl.BlockSpec((tile, share), lambda i, s, mask=mask: (i, s[0] ^ mask)) for mask in masks
    ]
    return [rows] * len(masks), specs


def piece_lines(pieces, tile, masks):
    share = pieces[0].shape[1]
    spec = pl.BlockSpec((tile, share), lambda i, s: (i, 0))
    return [pieces[mask] for mask in masks], [spec] * len(masks)


def side_specs(sides):
    return [pl.BlockSpec(side.shape, lambda i, s: (0, 0, 0)) for side in sides]


def call(kernel, steps, scalars, operands, specs, out_shape, out_spec, **more):
    scratch = more.pop("scratch_shapes", ())
    return pl.pallas_call(
        kernel,
        grid_spec=pltpu.PrefetchScalarGridSpec(
            num_scalar_prefetch=1,
            grid=(steps,),
            in_specs=specs,
            out_specs=out_spec,
            scratch_shapes=scratch,
        ),
        out_shape=out_shape,
        **more,
    )(scalars, *operands)


def accumulate_kernel(count, fresh, scalars, *refs):
    lines, sides, out_ref = refs[:count], refs[count : 2 * count], refs[-1]
    for which in range(2):
        total = summed(lines, sides, which)
        out_ref[which] = total if fresh else refs[2 * count][which] + total


def accumulate(scalars, height, tile, lines, sides, earlier=None):
    arrays, specs = lines
    width = sides[0].shape[2]
    total = pl.BlockSpec((2, tile, width), lambda i, s: (0, i, 0))
    count = len(arrays)
    more = [] if earlier is None else [earlier]
    return call(
        functools.partial(accumulate_kernel, count, earlier is None),
        height // tile,
        scalars,
        [*arrays, *sides, *more],
        specs + side_specs(sides) + [total] * len(more),
        jax.ShapeDtypeStruct((2, height, width), jnp.float32),
        total,
        input_output_aliases={2 * count + 1: 0} if more else {},
    )


def inverse_kernel(size, scale, count, scalars, *refs):
    lines, sides = refs[:count], refs[count : 2 * count]
    total_ref, out_ref, work, line = refs[2 * count :]
    order = out_ref.shape[1]
    gram = (
        (total_ref[0] + summed(lines, sides, 0)) * (total_ref[1] + summed(lines, sides, 1)) * scale
    )
    work[:, :order] = (gram + gram.T) * 0.5
    work[:, order:] = jnp.where(
        lax.broadcasted_iota(jnp.int32, (order, order), 0)
        == lax.broadcasted_iota(jnp.int32, (order, order), 1),
        1.0,
        0.0,
    ).astype(jnp.float32)
    for start in range(0, order, size):
        stop = start + size
        inverse = eliminate(work[start:stop, start:stop])
        line[:, start : order + stop] = dot(
            inverse, work[start:stop, start : order + stop], NN, HIGHEST
        )
        out_ref[0, start:stop, :stop], out_ref[1, start:stop, :stop] = halves(
            line[:, order : order + stop]
        )
        if stop < order:
            out_ref[:, start:stop, stop:] = jnp.zeros((2, size, order - stop), out_ref.dtype)
            work[stop:, stop : order + stop] -= dot(
                line[:, stop:order], line[:, stop : order + stop], TN, HIGHEST
            )


def factor_inverse(scalars, total, lines, sides, scale):
    size = 128
    arrays, specs = lines
    order = sides[0].shape[2]
    return call(
        functools.partial(inverse_kernel, size, scale, len(arrays)),
        1,
        scalars,
        [*arrays, *sides, total],
        specs + side_specs(sides + [total]),
        jax.ShapeDtypeStruct((2, order, order), jnp.bfloat16),
        pl.BlockSpec((2, order, order), lambda i, s: (0, 0, 0)),
        scratch_shapes=[
            pltpu.VMEM((order, 2 * order), jnp.float32),
            pltpu.VMEM((size, 2 * order), jnp.float32),
        ],
        cost_estimate=pl.CostEstimate(
            flops=15_000_000_000, transcendentals=order, bytes_accessed=8 * order * order
        ),
    )


def project_kernel(scale, count, fresh, scalars, *refs):
    lines, sides = refs[:count], refs[count : 2 * count]
    inverse_ref, out_ref = refs[2 * count], refs[-1]
    parts = [summed(lines, sides, which) for which in range(2)]
    if not fresh:
        parts = [part + refs[2 * count + 1][which] for which, part in enumerate(parts)]
    left = halves(parts[0] * parts[1] * scale)
    half = inverse_ref.shape[1] // 2
    low = dot_halves(
        [v[:, :half] for v in left], [inverse_ref[q, :half, :half] for q in range(2)], NT
    )
    high = dot_halves(left, [inverse_ref[q, half:, :] for q in range(2)], NT)
    if len(out_ref.shape) == 2:
        out_ref[:, :half] = low
        out_ref[:, half:] = high
    else:
        out_ref[0, :, :half], out_ref[1, :, :half] = halves(low)
        out_ref[0, :, half:], out_ref[1, :, half:] = halves(high)


def project(scalars, height, tile, lines, sides, inverse, scale, split, earlier=None):
    arrays, specs = lines
    width = sides[0].shape[2]
    count = len(arrays)
    both = pl.BlockSpec((2, tile, width), lambda i, s: (0, i, 0))
    more = [] if earlier is None else [earlier]
    if split:
        out = jax.ShapeDtypeStruct((2, height, width), jnp.bfloat16), both
    else:
        out = (
            jax.ShapeDtypeStruct((height, width), jnp.float32),
            pl.BlockSpec((tile, width), lambda i, s: (i, 0)),
        )
    return call(
        functools.partial(project_kernel, scale, count, earlier is None),
        height // tile,
        scalars,
        [*arrays, *sides, inverse, *more],
        specs + side_specs(sides + [inverse]) + [both] * len(more),
        *out,
    )


def update_kernel(scale, count, scalars, *refs):
    lines, sides = refs[:count], refs[count : 2 * count]
    panel_ref, solved_ref, out_ref = refs[2 * count :]
    slab = summed(lines, sides, 0) * summed(lines, sides, 1) * scale
    panel = panel_ref[...]
    trailing = slab - dot_halves(halves(panel), [solved_ref[q] for q in range(2)], NT)
    out_ref[...] = jnp.where(scalars[1] == 0, panel, trailing)


def update(scalars, height, tile, lines, sides, panel, solved, scale):
    arrays, specs = lines
    width = sides[0].shape[2]
    tiles = pl.BlockSpec((tile, width), lambda i, s: (i, 0))
    return call(
        functools.partial(update_kernel, scale, len(arrays)),
        height // tile,
        scalars,
        [*arrays, *sides, panel, solved],
        specs + side_specs(sides) + [tiles] + side_specs([solved]),
        jax.ShapeDtypeStruct((height, width), jnp.float32),
        tiles,
    )


def per_device(row_vectors, col_vectors, primal_matrix, dual_inverse):
    count = lax.axis_size("wide")
    me = lax.axis_index("wide")
    share, cone_order = primal_matrix.shape
    height = row_vectors.shape[0]
    order = col_vectors.shape[0]
    tile = 256
    scale = 16.0 / (cone_order * cone_order)
    scalars = jnp.stack([me, lax.axis_index("narrow")]).astype(jnp.int32)
    early, late, every = range(2, count - 2), range(count - 2, count), range(count)

    if share % 128:
        primal_matrix, dual_inverse = (
            jnp.concatenate(
                [
                    lax.dynamic_slice_in_dim(value, (me ^ mask) * share, share, 1)
                    for mask in every
                ],
                axis=1,
            )
            for value in (primal_matrix, dual_inverse)
        )

    def rows(masks):
        return row_lines(row_vectors, scalars, share, tile, masks)

    panel = from_first(col_vectors)
    columns = gather_pieces(col_vectors, count)
    panel = after(panel, *columns)
    own = products(scalars, primal_matrix, dual_inverse, columns)
    panels = gather_pieces(panel, count)
    first = products(scalars, primal_matrix, dual_inverse, [after(panels[0], own), *panels[1:]])

    masks = sorted(range(2, count, 2), key=lambda m: (bin(m).count("1"), m))
    firsts = [first] + [None] * (count - 1)
    firsts[1] = swap(first, 1, count)
    begun = False
    for mask in masks:
        if bin(mask).count("1") > 1 and not begun:
            begun = True
            start = accumulate(scalars, height, tile, rows((0, 1)), firsts[:2])
            total = accumulate(
                scalars, order, tile, piece_lines(panels, tile, (0, 1)), firsts[:2]
            )
            for bit in masks:
                if bin(bit).count("1") == 1:
                    firsts[bit] = after(firsts[bit], start, total)
                    firsts[bit + 1] = swap(firsts[bit], 1, count)
        firsts[mask] = forward(firsts, mask, count)
    for mask in masks:
        if firsts[mask + 1] is None and mask != count - 2:
            firsts[mask + 1] = swap(firsts[mask], 1, count)
    total = accumulate(
        scalars, order, tile, piece_lines(panels, tile, early), firsts[2:-2], total
    )
    firsts[-2] = after(firsts[-2], total)
    firsts[-1] = swap(firsts[-2], 1, count)

    owns = [own] + [None] * (count - 1)
    delayed = after(own, firsts[-2])
    for mask in range(2, count, 2):
        owns[mask] = swap(delayed, mask, count)
    owns[1] = swap(delayed, 1, count)
    inverse = factor_inverse(scalars, total, piece_lines(panels, order, late), firsts[-2:], scale)
    for mask in range(2, count, 2):
        owns[mask + 1] = swap(after(owns[mask], inverse), 1, count)

    solved = project(
        scalars, order, tile, piece_lines(columns, tile, every), firsts, inverse, scale, True
    )
    panel_cols = project(
        scalars,
        height,
        2 * tile,
        row_lines(row_vectors, scalars, share, 2 * tile, range(2, count)),
        firsts[2:],
        inverse,
        scale,
        False,
        start,
    )
    return update(scalars, height, tile, rows(every), owns, panel_cols, solved, scale)


def solution(mesh):
    placed = (P("wide", None), P("narrow", "wide"), P("wide", None), P("wide", None))
    return jax.shard_map(
        per_device, mesh=mesh, in_specs=placed, out_specs=P("wide", "narrow"), check_vma=False
    )
```
